32 devices in a mesh: ops: 8 (over z, x), wf: 4 (over y, core).
Axes of the slice: x: 2, y: 2, z: 4, core: 2. Of those that a mesh axis runs over, the one named last changes fastest.
Arguments:
- left_ops: bfloat16 [1024, 16, 1024], P('wf', 'ops'), may hold values from -6 to 6
- normal_right: bfloat16 [1024, 16, 1024], P('wf', 'ops'), may hold values from -0.1875 to 0.1875
- wavefunction: bfloat16 [1024, 1024], P(('ops', 'wf')), may hold values from -6 to 6
- rotation: bfloat16 [1024, 1024], replicated, may hold values from -0.1875 to 0.1875
- integrals: bfloat16 [16, 16], replicated, may hold values from -0.01171875 to 0.01171875
Outputs:
- sigma_vector: bfloat16 [1024, 1024], P('wf', 'ops')
- rotated_left: bfloat16 [1024, 16, 1024], P('wf', 'ops')
The draws below stay inside these ranges and needn't reach their ends.
All inputs are finite; a program needn't handle non-finite values.
Results may differ from the reference program's by a relative error of at most 0.012.
Values may be sent and summed in bfloat16 or wider, within the bound.
No kernel may reach another device: no remote copies, remote signals or barrier semaphores. Data moves between devices by JAX's collectives and lax.ppermute only.
A program may use at most 64 MiB of HBM per device.

```python
import jax
import jax.numpy as jnp
from jax import lax

M = 1024
OPS = 16


def steps_of(rng, dims, split, low, largest):
    level = 1.0
    for dim, shards_of in split:
        heights = jax.random.uniform(jax.random.fold_in(jax.random.fold_in(rng, 6), dim), (shards_of,), jnp.float32, low / len(split), largest / len(split))
        level = level * jnp.repeat(jnp.exp(heights), dims[dim] // shards_of).reshape((-1,) + (1,) * (len(dims) - 1 - dim))
    return level


def bell_draw(rng, extent, width, limit, split=(), kind=jnp.bfloat16):
    level = steps_of(rng, extent, split, -0.22, 0.18) if split else 1.0
    values = jax.random.normal(rng, extent, jnp.float32) * width * level
    return jnp.minimum(jnp.maximum(values, -limit), limit).astype(kind)


def setup_inputs(seed: int = 0) -> dict:
    streams_of = jax.random.split(jax.random.key(seed), 6)
    left_ops = bell_draw(streams_of[0], (M, OPS, M), 1.0, 6.0, ((0, 4), (1, 8)))
    normal_right = bell_draw(streams_of[1], (M, OPS, M), M ** -0.5, 0.1875, ((0, 4), (1, 8)))
    wavefunction = bell_draw(streams_of[2], (M, M), 1.0, 6.0, ((0, 32),))
    rotation = bell_draw(streams_of[3], (M, M), M ** -0.5, 0.1875)
    integrals = bell_draw(streams_of[4], (OPS, OPS), (OPS * OPS * M) ** -0.5, 0.01171875)
    return dict(left_ops=left_ops, normal_right=normal_right, wavefunction=wavefunction, rotation=rotation, integrals=integrals)


def reference(left_ops, normal_right, wavefunction, rotation, integrals):
    complement = jnp.einsum("kj,rjc->rkc", integrals.astype(jnp.float32), normal_right.astype(jnp.float32)).astype(jnp.bfloat16)

    def per_operator(carry, index):
        left_one = lax.dynamic_index_in_dim(left_ops, index, 1, keepdims=False)
        comp_one = lax.dynamic_index_in_dim(complement, index, 1, keepdims=False)
        projected = jnp.dot(left_one, wavefunction, preferred_element_type=jnp.float32).astype(jnp.bfloat16)
        carry = carry + jnp.dot(projected, comp_one, preferred_element_type=jnp.float32)
        halfway = jnp.dot(left_one, rotation, preferred_element_type=jnp.float32).astype(jnp.bfloat16)
        turned = jnp.dot(rotation.T, halfway, preferred_element_type=jnp.float32).astype(jnp.bfloat16)
        return carry, turned

    start_sum = jnp.zeros((M, M), jnp.float32)
    sigma_sum, turned_all = lax.scan(per_operator, start_sum, jnp.arange(OPS, dtype=jnp.int32))
    return sigma_sum.astype(jnp.bfloat16), jnp.transpose(turned_all, (1, 0, 2))
```

```python
import functools

import jax
import jax.numpy as jnp
from jax import lax
from jax.experimental import pallas as pl
from jax.experimental.pallas import tpu as pltpu
from jax.sharding import PartitionSpec as P


F32 = jnp.float32
BF16 = jnp.bfloat16
GROUP = 16
LANES = 128


def general(left_ops, normal_right, wavefunction, rotation, integrals):
    local_rows, op_count, full_width = left_ops.shape
    w_index = lax.axis_index("wf")
    left_flat = left_ops.reshape(local_rows * op_count, full_width)
    projected = jnp.dot(
        left_flat,
        lax.all_gather(wavefunction, ("ops", "wf"), axis=0, tiled=True),
        preferred_element_type=F32,
    )
    projected = projected.astype(BF16).reshape(local_rows, op_count, full_width)
    mixed_ops = jnp.einsum(
        "kj,ijc->ikc",
        integrals,
        lax.all_to_all(normal_right, "ops", split_axis=0, concat_axis=1, tiled=True),
        preferred_element_type=F32,
    ).astype(BF16)
    complement = lax.all_to_all(mixed_ops, "ops", split_axis=1, concat_axis=0, tiled=True)
    partial_sigma = lax.dot_general(
        projected,
        lax.all_gather(complement, "wf", axis=0, tiled=True),
        (((1, 2), (1, 0)), ((), ())),
        preferred_element_type=F32,
    )
    sigma_vector = lax.psum_scatter(partial_sigma, "ops", scatter_dimension=1, tiled=True)
    halfway = jnp.dot(left_flat, rotation, preferred_element_type=F32).astype(BF16)
    halfway = halfway.reshape(local_rows, op_count * full_width)
    own_cols = lax.dynamic_slice_in_dim(rotation, w_index * local_rows, local_rows, 1)
    rotated = lax.dot_general(
        own_cols,
        lax.all_gather(halfway, "wf", axis=0, tiled=True),
        (((0,), (0,)), ((), ())),
        preferred_element_type=F32,
    )
    rotated = rotated.reshape(local_rows, op_count, full_width)
    return sigma_vector.astype(BF16), rotated.astype(BF16)


def call(body, out_shape, args, scratch=()):
    vmem = pl.BlockSpec(memory_space=pltpu.VMEM)
    return pl.pallas_call(
        body,
        out_shape=out_shape,
        in_specs=[vmem] * len(args),
        out_specs=jax.tree.map(lambda _: vmem, out_shape),
        scratch_shapes=list(scratch),
    )(*args)


def order_rows(n_o, n_w, own_ref, other_ref, out_ref, whole, turned):
    o, w = lax.axis_index("ops"), lax.axis_index("wf")
    blocks, rows, cols = own_ref.shape
    for low in range(2):
        src = (own_ref, other_ref)[low]
        for e in range(blocks):
            high, ops_bits = e % 2, e // 2
            flip_o = sum(((ops_bits >> b) & 1) << (n_o.bit_length() - 2 - b) for b in range(n_o.bit_length() - 1))
            at = ((o ^ flip_o) * n_w + (w ^ (2 * high + low))) * rows
            whole[pl.ds(pl.multiple_of(at, rows), rows), :] = src[e]
    turned[...] = whole[...].T
    part = cols // 2
    sub = part // n_o
    for d in range(n_o):
        for low in range(2):
            at = ((w % 2) ^ low) * part + (o ^ d) * sub
            to = (2 * d + low) * sub
            out_ref[to : to + sub, :] = turned[pl.ds(pl.multiple_of(at, sub), sub), :]


def mix(n_o, weights_ref, *refs):
    o = lax.axis_index("ops")
    out_ref, stacked = refs[-2:]
    blocks = refs[:-2]
    pair, sub, width = blocks[0].shape
    size = n_o * pair * GROUP
    part = width // n_o
    for g in range(sub // GROUP):
        for d in range(n_o):
            for j in range(pair):
                at = (d * pair + j) * GROUP
                stacked[at : at + GROUP, :] = blocks[d][j, g * GROUP : (g + 1) * GROUP, :]
        mixed = jnp.dot(weights_ref[...], stacked[...], preferred_element_type=F32)
        mixed = mixed.astype(BF16)
        for b in range(n_o):
            at = pl.multiple_of((o ^ b) * part, part)
            out_ref[pl.ds(at, part), g * size : (g + 1) * size] = mixed[:, b * part : (b + 1) * part].T


def contract(n_o, added, own_ref, other_ref, *refs):
    out_ref, stacked = refs[-2:]
    blocks = refs[: n_o]
    rows, lanes = blocks[0].shape
    sub, cols = rows // 2, stacked.shape[1]
    pair = lanes // cols
    at = 0
    for low in range(2):
        for g in range(sub // GROUP):
            for d in range(n_o):
                for k in range(pair):
                    top = low * sub + g * GROUP
                    stacked[at : at + GROUP, :] = blocks[d][top : top + GROUP, k * cols : (k + 1) * cols]
                    at += GROUP
    half = at // 2
    total = jnp.dot(own_ref[...], stacked[:half, :], preferred_element_type=F32)
    total += jnp.dot(other_ref[...], stacked[half:, :], preferred_element_type=F32)
    if added:
        total += refs[n_o][...].astype(F32)
    out_ref[...] = total.astype(BF16)


def finish(*refs):
    out_ref = refs[-1]
    total = refs[0][...].astype(F32)
    for ref in refs[1:-1]:
        total += ref[...].astype(F32)
    out_ref[...] = total.T.astype(BF16)


def rotate(turned_ref, rotation_ref, *refs):
    w = lax.axis_index("wf")
    out_ref = refs[-1]
    lefts = refs[:-1]
    pair, rows, _ = lefts[0].shape
    for k in range(pair):
        half = None
        for e, left in enumerate(lefts):
            at = pl.multiple_of((w ^ e) * rows, rows)
            term = jnp.dot(turned_ref[:, pl.ds(at, rows)], left[k], preferred_element_type=F32)
            half = term if half is None else half + term
        out_ref[k] = jnp.dot(
            half.astype(BF16), rotation_ref[...], preferred_element_type=F32
        ).astype(BF16)


def fast(n_o, n_w, left_ops, normal_right, wavefunction, rotation, integrals):
    rows, pair, width = left_ops.shape
    o, w = lax.axis_index("ops"), lax.axis_index("wf")
    half = n_o // 2
    sub = rows // n_o
    part = width // n_o

    def flip_o(x, mask):
        return lax.ppermute(x, "ops", [(i, i ^ mask) for i in range(n_o)])

    def flip_w(x, mask):
        return lax.ppermute(x, "wf", [(i, i ^ mask) for i in range(n_w)])

    def exchange(blocks):
        crossed = flip_o(jnp.stack(blocks[half:]), half)
        got = [blocks[0]] + [None] * (n_o - 1)
        got[half] = crossed[0]
        for e in range(1, half):
            both = flip_o(jnp.stack([blocks[e], crossed[e]]), e)
            got[e], got[e + half] = both[0], both[1]
        return got

    wide = width // 2
    high = w // 2
    psi = lax.dynamic_slice_in_dim(wavefunction, high * wide, wide, 1)[None]
    away = lax.dynamic_slice_in_dim(wavefunction, (1 - high) * wide, wide, 1)[None]
    psi = jnp.concatenate([psi, flip_w(away, 2)])
    mask = half
    while mask:
        psi = jnp.concatenate([psi, flip_o(psi, mask)])
        mask //= 2
    psi_other = flip_w(psi, 1)

    left = jnp.transpose(left_ops, (1, 0, 2))
    left_y = flip_w(left, 2)
    left_c = flip_w(left, 1)
    left_cy = flip_w(left_y, 1)

    right = jnp.transpose(normal_right, (1, 0, 2))
    blocks = [lax.dynamic_slice_in_dim(right, (o ^ d) * sub, sub, 1) for d in range(n_o)]
    blocks = exchange(blocks)
    order = (jnp.arange(n_o) ^ o)[:, None] * pair + jnp.arange(pair)[None, :]
    pick = (order.reshape(-1, 1) == jnp.arange(n_o * pair)[None, :]).astype(BF16)
    mixing = jnp.dot(pick, jnp.dot(integrals, pick.T, preferred_element_type=F32).astype(BF16), preferred_element_type=F32)
    weights = jnp.kron(mixing.astype(BF16), jnp.eye(GROUP, dtype=BF16))
    size = n_o * pair * GROUP
    comp = call(
        functools.partial(mix, n_o),
        jax.ShapeDtypeStruct((width, n_o * pair * sub), BF16),
        [weights, *blocks],
        [pltpu.VMEM((size, width), BF16)],
    )
    comp_other = flip_w(comp, 1)

    psi_t = call(
        functools.partial(order_rows, n_o, n_w),
        jax.ShapeDtypeStruct((wide, width), BF16),
        [psi, psi_other],
        [pltpu.VMEM((width, wide), BF16), pltpu.VMEM((wide, width), BF16)],
    )

    def project(some_left):
        out = lax.dot_general(
            psi_t,
            some_left.reshape(pair * rows, width),
            (((1,), (1,)), ((), ())),
            preferred_element_type=F32,
        ).astype(BF16)
        out = out.reshape(n_o, 2 * sub, pair * rows)
        return exchange([out[d] for d in range(n_o)])

    def sigma_part(blocks, *more):
        return call(
            functools.partial(contract, n_o, len(more)),
            jax.ShapeDtypeStruct((width, rows), BF16),
            [comp, comp_other, *blocks, *more],
            [pltpu.VMEM((2 * n_o * pair * sub, rows), BF16)],
        )

    far = sigma_part(project(left_y))
    far = flip_w(far, 2)
    near = sigma_part(project(left), far).reshape(n_o, part, rows)
    pieces = [near[0]] + [flip_o(near[d], d) for d in range(1, n_o)]
    sigma = call(finish, jax.ShapeDtypeStruct((rows, part), BF16), pieces)

    own_cols = lax.dynamic_slice_in_dim(rotation, w * rows, rows, 1).T
    rotated = call(
        rotate,
        jax.ShapeDtypeStruct((pair, rows, width), BF16),
        [own_cols, rotation, left, left_c, left_y, left_cy],
    )
    return sigma, jnp.transpose(rotated, (1, 0, 2))


def solution(mesh):
    n_o, n_w = mesh.shape["ops"], mesh.shape["wf"]

    def local(left_ops, normal_right, wavefunction, rotation, integrals):
        rows, pair, width = left_ops.shape
        aligned = rows % (n_o * GROUP) == 0 and width % (n_o * LANES) == 0 and rows % LANES == 0
        if aligned and n_o >= 2 and n_o & (n_o - 1) == 0 and n_w == 4 and wavefunction.shape[0] % GROUP == 0:
            return fast(n_o, n_w, left_ops, normal_right, wavefunction, rotation, integrals)
        return general(left_ops, normal_right, wavefunction, rotation, integrals)

    placed = (P("wf", "ops", None), P("wf", "ops", None), P(("ops", "wf"), None), P(), P())
    return jax.shard_map(
        local,
        mesh=mesh,
        in_specs=placed,
        out_specs=(P("wf", "ops"), P("wf", "ops", None)),
        check_vma=False,
    )
```
